256 devices in a mesh: occ: 16 (over x_hi, y, core), ao: 16 (over x_lo, z).
Axes of the slice: x: 4 (x_hi: 2, x_lo: 2; x = x_hi * 2 + x_lo), y: 4, z: 8, core: 2. Of those that a mesh axis runs over, the one named last changes fastest.
Arguments:
- coef: bfloat16 [8192, 16], P('ao', 'occ'), may hold values from -0.25 to 0.25
- half_ints: bfloat16 [16, 1024, 8192], P('occ', None, 'ao'), may hold values from -0.5 to 0.5
- metric_inv: bfloat16 [64, 128, 128], replicated, may hold values from -1 to 2, as said below
- dom_blocks: int32 [16, 8], P('occ'), may hold values from 0 to 63, as said below
- dom_len: int32 [16], P('occ'), may hold values from 2 to 8
Outputs:
- exchange_k: float32 [8192, 8192], P('ao', 'occ')
- fit_density: float32 [8192], replicated
The draws below stay inside these ranges and needn't reach their ends.
Inputs may be any that keep to these rules, and one draw needn't show every extreme that they name: `dom_blocks`: each row holds 8 different block numbers. `metric_inv`: full rank blocks.
All inputs are finite; a program needn't handle non-finite values.
Results may differ from the reference program's by a relative error of at most 0.0055.
Values may be sent and summed in bfloat16 or wider, within the bound.
A program may use at most 128 MiB of HBM per device.

```python
import math
import jax
import jax.numpy as jnp
from jax import lax

BLK = 128
DOMB = 8
NFITB = 64
DOM = 1024
NAO = 8192
NOCC = 16
NFIT = 8192


def draw_metric_inv(key, part):
    noise = jax.random.normal(key, (NFITB, BLK, BLK), jnp.float32)
    return (jnp.eye(BLK, dtype=jnp.float32)[None] + 0.6 * noise / math.sqrt(BLK)).astype(jnp.bfloat16)


def draw_dom_blocks(key, part):
    scores = jax.random.randint(jax.random.fold_in(key, 7), (NOCC, NFITB), 0, 1 << 20)
    scores = scores * NFITB + jnp.arange(NFITB, dtype=jnp.int32)[None, :]
    order = jnp.argsort(scores, axis=1, stable=True)
    return order[:, :DOMB].astype(jnp.int32)


def with_ends(array, stream_key, least, high):
    place = [jax.random.randint(jax.random.fold_in(stream_key, axis), (), 0, length) for axis, length in enumerate(array.shape)]
    longest = array.shape.index(max(array.shape))
    beside = place[:longest] + [(place[longest] + 1) % array.shape[longest]] + place[longest + 1:]
    return array.at[tuple(place)].set(least).at[tuple(beside)].set(high)


def levels(rng, shape, split, least, top_value):
    factor_of, own = 1.0, jax.random.fold_in(rng, 6)
    for position, shards_of in split:
        heights = jnp.exp(jax.random.uniform(jax.random.fold_in(own, position), (shards_of,), jnp.float32, least / len(split), top_value / len(split)))
        factor_of = factor_of * jnp.repeat(heights, shape[position] // shards_of).reshape([-1 if axis == position else 1 for axis in range(len(shape))])
    return factor_of


def normal_values(own_key, extent, deviation, most, shards=(), kind=jnp.bfloat16):
    array = deviation * jax.random.normal(own_key, extent, jnp.float32)
    if shards:
        array = array * levels(own_key, extent, shards, -0.22, 0.18)
    return jnp.clip(array, -most, most).astype(kind)


def setup_inputs(seed: int = 0) -> dict:
    keys = jax.random.split(jax.random.key(seed), 6)
    return {
        "coef": normal_values(keys[0], (NAO, NOCC), (NAO // 16) ** -0.5, 0.25, ((0, 16), (1, 16))),
        "half_ints": normal_values(keys[1], (NOCC, DOM, NAO), 0.084, 0.5, ((0, 16), (2, 16))),
        "metric_inv": draw_metric_inv(jax.random.fold_in(keys[5], 71), 0),
        "dom_blocks": draw_dom_blocks(jax.random.fold_in(keys[5], 71), 0),
        "dom_len": with_ends(jax.random.randint(keys[4], (NOCC,), DOMB // 4, DOMB + 1), jax.random.fold_in(keys[4], 1), DOMB // 4, DOMB).astype(jnp.int32),
    }


def fit_one(ints_one, blocks_one, length_one, metric_inv):
    metric_rows = metric_inv[blocks_one].astype(jnp.float32)
    raw_ints = ints_one.reshape(DOMB, BLK, NAO).astype(jnp.float32)
    fitted = jnp.einsum('sab,sbm->sam', metric_rows, raw_ints)
    live_slots = jnp.arange(DOMB, dtype=jnp.int32) < length_one
    fitted = jnp.where(live_slots[:, None, None], fitted, 0.0)
    return fitted.reshape(DOM, NAO).astype(jnp.bfloat16)


def reference(coef, half_ints, metric_inv, dom_blocks, dom_len):
    fitted = lax.map(lambda item: fit_one(item[0], item[1], item[2], metric_inv), (half_ints, dom_blocks, dom_len))
    fitted_wide = fitted.astype(jnp.float32)
    pair_sum = jnp.einsum('ipm,mi->ip', fitted_wide, coef.astype(jnp.float32))
    one_hot = (dom_blocks[:, :, None] == jnp.arange(NFITB, dtype=jnp.int32)[None, None, :]).astype(jnp.float32)
    density = jnp.einsum('isf,isr->fr', one_hot, pair_sum.reshape(NOCC, DOMB, BLK)).reshape(NFIT)
    stacked = fitted_wide.reshape(NOCC * DOM, NAO)
    exchange_k = jnp.dot(stacked.T, stacked, preferred_element_type=jnp.float32)
    return exchange_k, density
```

```python
import jax
import jax.numpy as jnp
from jax import lax
from jax.experimental import pallas as pl
from jax.experimental.pallas import tpu as pltpu
from jax.sharding import PartitionSpec as P

MESH = pl.DeviceIdType.MESH
F32, BF16 = jnp.float32, jnp.bfloat16
RING = 8
CHUNKS = 4
CLASSES = (
    (0, 0, 0, False),
    (0, 1, 0, True),
    (-1, 1, 0, True),
    (1, 1, 1, False),
    (0, 1, 1, True),
    (-1, 1, 1, True),
    (-1, 2, 0, True),
    (-2, 1, 1, True),
    (-2, 2, 0, False),
    (-2, 2, 1, False),
)
EARLY = 6
NT = (((1,), (1,)), ((), ()))


def slot_of(offset, other):
    return offset + 4 if other else offset + 2


def wait_for(ref, sem):
    pltpu.make_async_copy(ref, ref, sem).wait()


def kernel(
    blocks_ref, len_ref, coef_ref, ints_ref, metric_ref,
    out_ref, dens_ref,
    held, give, core_in, local, summed, first_in, last_in, final, owned, pair_in, term_in,
    own_sem, pass_sem, chunk_sem, core_send, core_recv, sum_send, sum_recv,
    end_send, end_recv, pair_send, pair_recv, term_send, term_recv,
):
    occ, ao = lax.axis_index("occ"), lax.axis_index("ao")
    col, z = ao // RING, lax.rem(ao, RING)
    core, spot = lax.rem(occ, 2), occ // 2
    n_spots = RING
    width = held.shape[1]
    block = metric_ref.shape[1]
    slots = held.shape[2] // block
    rows = width // CHUNKS
    half = width // 2
    strip = half // n_spots

    def ao_at(c, dz):
        return c * RING + lax.rem(z + dz + RING, RING)

    up, down, across = ao_at(col, 1), ao_at(col, -1), ao_at(1 - col, 0)

    def chunk(slot, k):
        return held.at[slot, pl.ds(k * rows, rows), :]

    def send_chunk(src_slot, dst_slot, k, send_sem, to):
        pltpu.make_async_remote_copy(
            src_ref=chunk(src_slot, k), dst_ref=chunk(dst_slot, k), send_sem=send_sem,
            recv_sem=chunk_sem.at[dst_slot, k], device_id={"occ": occ, "ao": to}, device_id_type=MESH,
        ).start()

    def wait_chunk(slot, k):
        wait_for(chunk(slot, k), chunk_sem.at[slot, k])

    for k in range(CHUNKS):
        for s in range(slots):
            value = lax.dot_general(
                metric_ref[blocks_ref[0, s]], ints_ref[pl.ds(s * block, block), pl.ds(k * rows, rows)],
                (((1,), (0,)), ((), ())), preferred_element_type=F32,
            )
            live = jnp.full(value.shape, len_ref[0], jnp.int32) > s
            value = jnp.where(live, value, 0.0)
            held[2, pl.ds(k * rows, rows), pl.ds(s * block, block)] = value.T.astype(BF16)
        send_chunk(2, 1, k, own_sem.at[0], up)
        send_chunk(2, 3, k, own_sem.at[1], down)

    pair = lax.dot_general(
        coef_ref[...], held[2], (((1,), (0,)), ((), ())), preferred_element_type=F32
    )
    for s in range(slots):
        pair_in[ao, pl.ds(s, 1), :] = pair[0:1, s * block : (s + 1) * block]
    n_ao = pair_in.shape[0]
    for k in range(1, n_ao):
        pltpu.make_async_remote_copy(
            src_ref=pair_in.at[ao], dst_ref=pair_in.at[ao], send_sem=pair_send, recv_sem=pair_recv,
            device_id={"occ": occ, "ao": lax.rem(ao + k, n_ao)}, device_id_type=MESH,
        ).start()

    for k in range(CHUNKS):
        wait_chunk(1, k)
        send_chunk(1, 0, k, pass_sem.at[0], up)
        wait_chunk(3, k)
        send_chunk(3, 4, k, pass_sem.at[1], down)
        send_chunk(3, 5, k, pass_sem.at[2], across)

    wait_for(pair_in.at[pl.ds(0, n_ao - 1)], pair_recv)
    term = pair_in[0]
    for k in range(1, n_ao):
        term = term + pair_in[k]
    term_in[occ, pl.ds(0, slots), :] = term
    for s in range(slots):
        term_in[occ, pl.ds(slots + s, 1), :] = jnp.full((1, block), blocks_ref[0, s], jnp.int32).astype(F32)
    n_occ = term_in.shape[0]
    for k in range(1, n_occ):
        pltpu.make_async_remote_copy(
            src_ref=term_in.at[occ], dst_ref=term_in.at[occ], send_sem=term_send, recv_sem=term_recv,
            device_id={"occ": lax.rem(occ + k, n_occ), "ao": ao}, device_id_type=MESH,
        ).start()

    def product(c, which):
        i, t, other, _ = CLASSES[c]
        lhs = held[slot_of(i, 0), pl.ds(pl.multiple_of(which * half, half), half), :]
        return lax.dot_general(lhs, held[slot_of(t, other)], NT, preferred_element_type=F32)

    def for_other_core(c, g):
        give[c] = product(c, 1 - core).astype(BF16)
        pltpu.make_async_remote_copy(
            src_ref=give.at[c], dst_ref=core_in.at[c], send_sem=core_send.at[g], recv_sem=core_recv.at[g],
            device_id={"occ": occ + 1 - 2 * core, "ao": ao}, device_id_type=MESH,
        ).start()

    def sum_cores(lo, hi, g, arrived):
        n = hi - lo
        wait_for(core_in.at[pl.ds(lo, n)], core_recv.at[g])
        for c in range(lo, hi):
            summed[c] = (local[c] + core_in[c].astype(F32)).astype(BF16)
        for k in range(1, n_spots):
            peer = lax.rem(spot + k, n_spots)
            pltpu.make_async_remote_copy(
                src_ref=summed.at[pl.ds(lo, n), pl.ds(pl.multiple_of(peer * strip, strip), strip), :],
                dst_ref=arrived.at[k - 1], send_sem=sum_send.at[g], recv_sem=sum_recv.at[g],
                device_id={"occ": peer * 2 + core, "ao": ao}, device_id_type=MESH,
            ).start()

    place = pl.ds(pl.multiple_of((core * n_spots + spot) * strip, strip), strip)

    def deliveries(lo, hi):
        n = sum(1 + CLASSES[c][3] for c in range(lo))
        for c in range(lo, hi):
            i, t, other, both = CLASSES[c]
            first = ao_at(col, i)
            second = ao_at(1 - col if other else col, t)
            for occ_to, ao_to in ((second, first), (first, second))[: 1 + both]:
                yield n, c, occ_to, ao_to
                n += 1

    def deliver(lo, hi, g, arrived):
        n = hi - lo
        wait_for(arrived, sum_recv.at[g])
        for c in range(lo, hi):
            value = summed[c, pl.ds(pl.multiple_of(spot * strip, strip), strip), :].astype(F32)
            for k in range(n_spots - 1):
                value = value + arrived[k, c - lo].astype(F32)
            final[c] = value.astype(BF16)
        for m, c, occ_to, ao_to in deliveries(lo, hi):
            mine = jnp.logical_and(occ_to == occ, ao_to == ao)

            @pl.when(mine)
            def _():
                pltpu.make_async_copy(final.at[c], owned.at[place], end_recv).start()

            @pl.when(jnp.logical_not(mine))
            def _():
                pltpu.make_async_remote_copy(
                    src_ref=final.at[c], dst_ref=owned.at[place], send_sem=end_send.at[m], recv_sem=end_recv,
                    device_id={"occ": occ_to, "ao": ao_to}, device_id_type=MESH,
                ).start()

    n_classes = len(CLASSES)
    for c in range(3):
        for_other_core(c, 0)
    for k in range(CHUNKS):
        wait_chunk(5, k)
    for c in range(3, EARLY):
        for_other_core(c, 0)
    for c in range(EARLY):
        local[c] = product(c, core)
    sum_cores(0, EARLY, 0, first_in)

    for k in range(CHUNKS):
        wait_chunk(4, k)
        send_chunk(4, 6, k, pass_sem.at[3], across)
    for k in range(CHUNKS):
        wait_chunk(0, k)
    for c in range(EARLY, n_classes - 1):
        for_other_core(c, 1)
    for c in range(EARLY, n_classes - 1):
        local[c] = product(c, core)
    deliver(0, EARLY, 0, first_in)
    for k in range(CHUNKS):
        wait_chunk(6, k)
    for_other_core(n_classes - 1, 1)
    local[n_classes - 1] = product(n_classes - 1, core)
    sum_cores(EARLY, n_classes, 1, last_in)

    wait_for(term_in.at[pl.ds(0, n_occ - 1)], term_recv)
    terms = jnp.concatenate([term_in[i, 0:slots, :] for i in range(n_occ)], axis=0)
    numbers = jnp.concatenate([term_in[i, slots : 2 * slots, :] for i in range(n_occ)], axis=0)
    here = numbers == lax.broadcasted_iota(jnp.int32, numbers.shape, 1).astype(F32)
    full = lax.dot_general(
        here.astype(F32).T, terms, (((1,), (0,)), ((), ())),
        precision=lax.Precision.HIGHEST, preferred_element_type=F32,
    )
    dens_ref[...] = full[0 : dens_ref.shape[0]]

    deliver(EARLY, n_classes, 1, last_in)
    wait_for(owned, end_recv)
    turned = lax.rem(lax.rem(occ, RING) - z + RING, RING) > RING // 2

    @pl.when(turned)
    def _():
        out_ref[...] = owned[...].astype(F32).T

    @pl.when(jnp.logical_not(turned))
    def _():
        out_ref[...] = owned[...].astype(F32)

    wait_for(held.at[2], own_sem.at[0])
    wait_for(held.at[2], own_sem.at[1])
    for n in range(4):
        wait_for(held.at[0], pass_sem.at[n])
    wait_for(give.at[pl.ds(0, EARLY)], core_send.at[0])
    wait_for(give.at[pl.ds(EARLY, n_classes - EARLY)], core_send.at[1])
    wait_for(first_in, sum_send.at[0])
    wait_for(last_in, sum_send.at[1])
    wait_for(pair_in.at[pl.ds(0, n_ao - 1)], pair_send)
    wait_for(term_in.at[pl.ds(0, n_occ - 1)], term_send)
    for m, c, occ_to, ao_to in deliveries(0, n_classes):
        @pl.when(jnp.logical_not(jnp.logical_and(occ_to == occ, ao_to == ao)))
        def _():
            wait_for(final.at[c], end_send.at[m])


def on_device(coef, half_ints, metric_inv, dom_blocks, dom_len):
    _, domain, width = half_ints.shape
    fit_blocks, block, _ = metric_inv.shape
    slots = domain // block
    n = len(CLASSES)
    half, strip = width // 2, width // 2 // RING
    smem = pl.BlockSpec(memory_space=pltpu.SMEM)
    vmem = pl.BlockSpec(memory_space=pltpu.VMEM)
    dma = pltpu.SemaphoreType.DMA
    exchange, density = pl.pallas_call(
        kernel,
        out_shape=(
            jax.ShapeDtypeStruct((width, width), F32),
            jax.ShapeDtypeStruct((fit_blocks, block), F32),
        ),
        in_specs=[smem, smem, vmem, vmem, vmem],
        out_specs=(vmem, vmem),
        scratch_shapes=[
            pltpu.VMEM((7, width, domain), BF16),
            pltpu.VMEM((n, half, width), BF16),
            pltpu.VMEM((n, half, width), BF16),
            pltpu.VMEM((n, half, width), F32),
            pltpu.VMEM((n, half, width), BF16),
            pltpu.VMEM((RING - 1, EARLY, strip, width), BF16),
            pltpu.VMEM((RING - 1, n - EARLY, strip, width), BF16),
            pltpu.VMEM((n, strip, width), BF16),
            pltpu.VMEM((width, width), BF16),
            pltpu.VMEM((16, slots, block), F32),
            pltpu.VMEM((16, 2 * slots, block), F32),
            dma((2,)), dma((4,)), dma((7, CHUNKS)), dma((2,)), dma((2,)), dma((2,)), dma((2,)),
            dma((16,)), dma, dma, dma, dma, dma,
        ],
        compiler_params=pltpu.CompilerParams(vmem_limit_bytes=56 * 1024 * 1024, has_side_effects=True),
        cost_estimate=pl.CostEstimate(
            flops=n * 2 * width * width * domain, bytes_accessed=8 * 1024 * 1024, transcendentals=0
        ),
        name="exchange",
    )(dom_blocks, dom_len, coef.reshape(1, width), half_ints.reshape(domain, width), metric_inv)
    return exchange, density.reshape(fit_blocks * block)


def solution(mesh):
    in_specs = (P("ao", "occ"), P("occ", None, "ao"), P(), P("occ", None), P("occ"))
    out_specs = (P("ao", "occ"), P())
    return jax.shard_map(
        on_device, mesh=mesh, in_specs=in_specs, out_specs=out_specs, check_vma=False
    )
```

```python
import jax
import jax.numpy as jnp
from jax import lax
from jax.experimental import pallas as pl
from jax.experimental.pallas import tpu as pltpu
from jax.sharding import PartitionSpec as P

MESH = pl.DeviceIdType.MESH
F32, BF16 = jnp.float32, jnp.bfloat16
RING = 8
Y = 4
CHUNKS = 4
CLASSES = (
    (0, 0, 0, False),
    (0, 1, 0, True),
    (-1, 1, 0, True),
    (1, 1, 1, False),
    (0, 1, 1, True),
    (-1, 1, 1, True),
    (-2, 1, 0, True),
    (-2, 1, 1, True),
    (-2, 2, 0, False),
    (-2, 2, 1, False),
)
GROUPS = ((0, 1), (1, 3), (3, 6), (6, 9), (9, 10))
NT = (((1,), (1,)), ((), ()))


def slot_of(offset, other):
    return offset + 4 if other else offset + 2


def wait_for(ref, sem):
    pltpu.make_async_copy(ref, ref, sem).wait()


def kernel(
    blocks_ref, len_ref, coef_ref, ints_hbm, metric_hbm,
    out_ref, dens_ref,
    ints, metric, held, give, core_in, local, summed, y_in, y_sum, x_in, final, owned, pair_in, term_in,
    load_sem, own_sem, pass_sem, chunk_sem, core_send, core_recv, y_send, y_recv, x_send, x_recv,
    end_send, end_recv, pair_send, pair_recv, term_send, term_recv,
):
    occ, ao = lax.axis_index("occ"), lax.axis_index("ao")
    n_occ, n_ao = term_in.shape[0], pair_in.shape[0]
    barrier = pltpu.get_barrier_semaphore()
    for k in range(1, n_occ):
        pl.semaphore_signal(
            barrier, inc=1, device_id={"occ": lax.rem(occ + k, n_occ), "ao": ao}, device_id_type=MESH
        )
    for k in range(1, n_ao):
        pl.semaphore_signal(
            barrier, inc=1, device_id={"occ": occ, "ao": lax.rem(ao + k, n_ao)}, device_id_type=MESH
        )
    loads = (
        pltpu.make_async_copy(metric_hbm, metric, load_sem.at[0]),
        pltpu.make_async_copy(ints_hbm, ints, load_sem.at[1]),
    )
    for load in loads:
        load.start()

    col, z = ao // RING, lax.rem(ao, RING)
    core = lax.rem(occ, 2)
    y, x = lax.rem(occ // 2, Y), occ // (2 * Y)
    width, domain = held.shape[1], held.shape[2]
    block = metric.shape[1]
    slots = domain // block
    rows = width // CHUNKS
    half = width // 2
    part = half // Y
    strip = part // 2

    def ao_at(c, dz):
        return c * RING + lax.rem(z + dz + RING, RING)

    up, down, across = ao_at(col, 1), ao_at(col, -1), ao_at(1 - col, 0)

    def send(src, dst, send_sem, recv_sem, occ_to, ao_to):
        pltpu.make_async_remote_copy(
            src_ref=src, dst_ref=dst, send_sem=send_sem, recv_sem=recv_sem,
            device_id={"occ": occ_to, "ao": ao_to}, device_id_type=MESH,
        ).start()

    def chunk(slot, k):
        return held.at[slot, pl.ds(k * rows, rows), :]

    def send_chunk(src_slot, dst_slot, k, send_sem, to):
        send(chunk(src_slot, k), chunk(dst_slot, k), send_sem, chunk_sem.at[dst_slot, k], occ, to)

    def wait_chunk(slot, k):
        wait_for(chunk(slot, k), chunk_sem.at[slot, k])

    for load in loads:
        load.wait()
    for k in range(CHUNKS):
        for s in range(slots):
            value = lax.dot_general(
                metric[blocks_ref[0, s]], ints[pl.ds(s * block, block), pl.ds(k * rows, rows)],
                (((1,), (0,)), ((), ())), preferred_element_type=F32,
            )
            live = jnp.full(value.shape, len_ref[0], jnp.int32) > s
            value = jnp.where(live, value, 0.0)
            held[2, pl.ds(k * rows, rows), pl.ds(s * block, block)] = value.T.astype(BF16)
        if k == 0:
            pl.semaphore_wait(barrier, n_occ + n_ao - 2)
        send_chunk(2, 1, k, own_sem.at[0], up)
        send_chunk(2, 3, k, own_sem.at[1], down)

    def product(c, which):
        i, t, other, _ = CLASSES[c]
        lhs = held[slot_of(i, 0), pl.ds(pl.multiple_of(which * half, half), half), :]
        return lax.dot_general(lhs, held[slot_of(t, other)], NT, preferred_element_type=F32)

    def multiply(g):
        for c in range(*GROUPS[g]):
            give[c] = product(c, 1 - core).astype(BF16)
            send(give.at[c], core_in.at[c], core_send.at[g], core_recv.at[g], occ + 1 - 2 * core, ao)
        for c in range(*GROUPS[g]):
            local[c] = product(c, core)

    def span(g):
        lo, hi = GROUPS[g]
        return pl.ds(lo, hi - lo)

    def sum_cores(g):
        wait_for(core_in.at[span(g)], core_recv.at[g])
        for c in range(*GROUPS[g]):
            summed[c] = (local[c] + core_in[c].astype(F32)).astype(BF16)
        for k in (1, 3, 2):
            to = lax.rem(y + k, Y)
            send(
                summed.at[span(g), pl.ds(pl.multiple_of(to * part, part), part), :], y_in.at[k - 1, span(g)],
                y_send.at[g], y_recv.at[g], x * (2 * Y) + to * 2 + core, ao,
            )

    def sum_y(g):
        wait_for(y_in.at[:, span(g)], y_recv.at[g])
        for c in range(*GROUPS[g]):
            value = summed[c, pl.ds(pl.multiple_of(y * part, part), part), :].astype(F32)
            for k in range(Y - 1):
                value = value + y_in[k, c].astype(F32)
            y_sum[c] = value.astype(BF16)
        send(
            y_sum.at[span(g), pl.ds(pl.multiple_of((1 - x) * strip, strip), strip), :], x_in.at[span(g)],
            x_send.at[g], x_recv.at[g], (1 - x) * (2 * Y) + y * 2 + core, ao,
        )

    place = pl.ds(pl.multiple_of((core * (2 * Y) + y * 2 + x) * strip, strip), strip)

    def deliveries(lo, hi):
        n = sum(1 + CLASSES[c][3] for c in range(lo))
        for c in range(lo, hi):
            i, t, other, both = CLASSES[c]
            first = ao_at(col, i)
            second = ao_at(1 - col if other else col, t)
            for occ_to, ao_to in ((second, first), (first, second))[: 1 + both]:
                yield n, c, occ_to, ao_to
                n += 1

    def deliver(g):
        wait_for(x_in.at[span(g)], x_recv.at[g])
        for c in range(*GROUPS[g]):
            value = y_sum[c, pl.ds(pl.multiple_of(x * strip, strip), strip), :].astype(F32)
            final[c] = (value + x_in[c].astype(F32)).astype(BF16)
        for m, c, occ_to, ao_to in deliveries(*GROUPS[g]):
            mine = jnp.logical_and(occ_to == occ, ao_to == ao)

            @pl.when(mine)
            def _():
                pltpu.make_async_copy(final.at[c], owned.at[place], end_recv).start()

            @pl.when(jnp.logical_not(mine))
            def _():
                send(final.at[c], owned.at[place], end_send.at[m], end_recv, occ_to, ao_to)

    def pass_on(k):
        wait_chunk(1, k)
        send_chunk(1, 0, k, pass_sem.at[0], up)
        wait_chunk(3, k)
        send_chunk(3, 4, k, pass_sem.at[1], down)
        send_chunk(3, 5, k, pass_sem.at[2], across)

    def pass_across(k):
        wait_chunk(4, k)
        send_chunk(4, 6, k, pass_sem.at[3], across)

    pair = lax.dot_general(
        coef_ref[...], held[2], (((1,), (0,)), ((), ())), preferred_element_type=F32
    )
    for s in range(slots):
        pair_in[ao, pl.ds(s, 1), :] = pair[0:1, s * block : (s + 1) * block]
    for k in range(1, n_ao):
        send(pair_in.at[ao], pair_in.at[ao], pair_send, pair_recv, occ, lax.rem(ao + k, n_ao))

    multiply(0)
    pass_on(0)
    sum_cores(0)
    pass_on(1)

    wait_for(pair_in.at[pl.ds(0, n_ao - 1)], pair_recv)
    term = pair_in[0]
    for k in range(1, n_ao):
        term = term + pair_in[k]
    term_in[occ, pl.ds(0, slots), :] = term
    for s in range(slots):
        term_in[occ, pl.ds(slots + s, 1), :] = jnp.full((1, block), blocks_ref[0, s], jnp.int32).astype(F32)
    for k in range(1, n_occ):
        send(term_in.at[occ], term_in.at[occ], term_send, term_recv, lax.rem(occ + k, n_occ), ao)

    pass_on(2)
    sum_y(0)
    pass_on(3)
    multiply(1)
    sum_cores(1)
    for k in range(CHUNKS):
        wait_chunk(5, k)
    multiply(2)
    pass_across(0)
    sum_cores(2)
    deliver(0)
    pass_across(1)
    sum_y(1)
    pass_across(2)
    sum_y(2)
    pass_across(3)
    for k in range(CHUNKS):
        wait_chunk(0, k)
    multiply(3)
    sum_cores(3)
    deliver(1)
    for k in range(CHUNKS):
        wait_chunk(6, k)
    multiply(4)
    sum_cores(4)
    deliver(2)

    wait_for(term_in.at[pl.ds(0, n_occ - 1)], term_recv)
    terms = jnp.concatenate([term_in[i, 0:slots, :] for i in range(n_occ)], axis=0)
    numbers = jnp.concatenate([term_in[i, slots : 2 * slots, :] for i in range(n_occ)], axis=0)
    here = numbers == lax.broadcasted_iota(jnp.int32, numbers.shape, 1).astype(F32)
    full = lax.dot_general(
        here.astype(F32).T, terms, (((1,), (0,)), ((), ())),
        precision=lax.Precision.HIGHEST, preferred_element_type=F32,
    )
    dens_ref[...] = full[0 : dens_ref.shape[0]]

    sum_y(3)
    sum_y(4)
    deliver(3)
    deliver(4)
    wait_for(owned, end_recv)
    turned = lax.rem(lax.rem(occ, RING) - z + RING, RING) > RING // 2

    @pl.when(turned)
    def _():
        out_ref[...] = owned[...].astype(F32).T.astype(BF16)

    @pl.when(jnp.logical_not(turned))
    def _():
        out_ref[...] = owned[...]

    wait_for(held.at[2], own_sem.at[0])
    wait_for(held.at[2], own_sem.at[1])
    for n in range(4):
        wait_for(held.at[0], pass_sem.at[n])
    for g in range(len(GROUPS)):
        wait_for(give.at[span(g)], core_send.at[g])
        wait_for(y_in.at[:, span(g)], y_send.at[g])
        wait_for(x_in.at[span(g)], x_send.at[g])
    wait_for(pair_in.at[pl.ds(0, n_ao - 1)], pair_send)
    wait_for(term_in.at[pl.ds(0, n_occ - 1)], term_send)
    for m, c, occ_to, ao_to in deliveries(0, len(CLASSES)):
        @pl.when(jnp.logical_not(jnp.logical_and(occ_to == occ, ao_to == ao)))
        def _():
            wait_for(final.at[c], end_send.at[m])


def on_device(coef, half_ints, metric_inv, dom_blocks, dom_len):
    _, domain, width = half_ints.shape
    fit_blocks, block, _ = metric_inv.shape
    slots = domain // block
    n = len(CLASSES)
    half = width // 2
    part = half // Y
    smem = pl.BlockSpec(memory_space=pltpu.SMEM)
    vmem = pl.BlockSpec(memory_space=pltpu.VMEM)
    hbm = pl.BlockSpec(memory_space=pl.ANY)
    dma = pltpu.SemaphoreType.DMA
    per_group = dma((len(GROUPS),))
    exchange, density = pl.pallas_call(
        kernel,
        out_shape=(
            jax.ShapeDtypeStruct((width, width), BF16),
            jax.ShapeDtypeStruct((fit_blocks, block), F32),
        ),
        in_specs=[smem, smem, vmem, hbm, hbm],
        out_specs=(vmem, vmem),
        scratch_shapes=[
            pltpu.VMEM((domain, width), BF16),
            pltpu.VMEM((fit_blocks, block, block), BF16),
            pltpu.VMEM((7, width, domain), BF16),
            pltpu.VMEM((n, half, width), BF16),
            pltpu.VMEM((n, half, width), BF16),
            pltpu.VMEM((n, half, width), F32),
            pltpu.VMEM((n, half, width), BF16),
            pltpu.VMEM((Y - 1, n, part, width), BF16),
            pltpu.VMEM((n, part, width), BF16),
            pltpu.VMEM((n, part // 2, width), BF16),
            pltpu.VMEM((n, part // 2, width), BF16),
            pltpu.VMEM((width, width), BF16),
            pltpu.VMEM((16, slots, block), F32),
            pltpu.VMEM((16, 2 * slots, block), F32),
            dma((2,)), dma((2,)), dma((4,)), dma((7, CHUNKS)),
            per_group, per_group, per_group, per_group, per_group, per_group,
            dma((16,)), dma, dma, dma, dma, dma,
        ],
        compiler_params=pltpu.CompilerParams(
            vmem_limit_bytes=56 * 1024 * 1024, has_side_effects=True, collective_id=0
        ),
        cost_estimate=pl.CostEstimate(
            flops=n * 2 * width * width * domain, bytes_accessed=8 * 1024 * 1024, transcendentals=0
        ),
        name="exchange",
    )(dom_blocks, dom_len, coef.reshape(1, width), half_ints.reshape(domain, width), metric_inv)
    return exchange.astype(F32), density.reshape(fit_blocks * block)


def solution(mesh):
    in_specs = (P("ao", "occ"), P("occ", None, "ao"), P(), P("occ", None), P("occ"))
    out_specs = (P("ao", "occ"), P())
    return jax.shard_map(
        on_device, mesh=mesh, in_specs=in_specs, out_specs=out_specs, check_vma=False
    )
```

```python
import jax
import jax.numpy as jnp
from jax import lax
from jax.experimental import pallas as pl
from jax.experimental.pallas import tpu as pltpu
from jax.sharding import PartitionSpec as P

MESH = pl.DeviceIdType.MESH
F32, BF16 = jnp.float32, jnp.bfloat16
RING = 8
Y = 4
CHUNKS = 8
PLAN = (
    ((0, 0, 0, False, 0, 2),),
    ((0, 1, 0, True, 0, 2), (-1, 1, 0, True, 0, 2)),
    ((1, 1, 1, False, 0, 2), (0, 1, 1, True, 0, 2), (-1, 1, 1, True, 0, 2)),
    ((-2, 1, 0, True, 0, 1), (-2, 1, 1, True, 0, 1)),
    ((-2, 1, 0, True, 1, 1), (-2, 1, 1, True, 1, 1), "opposite"),
    ("across",),
)
UNITS, SENDS = 19, 22
NT = (((1,), (1,)), ((), ()))


def wait_for(ref, sem):
    pltpu.make_async_copy(ref, ref, sem).wait()


def kernel(
    blocks_ref, len_ref, coef_ref, ints_hbm, metric_hbm,
    out_ref, dens_ref,
    ints, metric, held, give, core_in, local, summed, y_in, y_sum, x_in, final, owned, pair_in, term_in,
    load_sem, own_sem, pass_sem, chunk_sem, core_send, core_recv, y_send, y_recv, x_send, x_recv,
    end_send, end_recv, pair_send, pair_recv, term_send, term_recv,
):
    occ, ao = lax.axis_index("occ"), lax.axis_index("ao")
    n_occ, n_ao = term_in.shape[0], pair_in.shape[0]
    barrier = pltpu.get_barrier_semaphore()
    for k in range(1, n_occ):
        pl.semaphore_signal(
            barrier, inc=1, device_id={"occ": lax.rem(occ + k, n_occ), "ao": ao}, device_id_type=MESH
        )
    for k in range(1, n_ao):
        pl.semaphore_signal(
            barrier, inc=1, device_id={"occ": occ, "ao": lax.rem(ao + k, n_ao)}, device_id_type=MESH
        )
    loads = (
        pltpu.make_async_copy(metric_hbm, metric, load_sem.at[0]),
        pltpu.make_async_copy(ints_hbm, ints, load_sem.at[1]),
    )
    for load in loads:
        load.start()

    col, z = ao // RING, lax.rem(ao, RING)
    core = lax.rem(occ, 2)
    y, x = lax.rem(occ // 2, Y), occ // (2 * Y)
    width, domain = held.shape[1], held.shape[2]
    block = metric.shape[1]
    slots = domain // block
    rows = width // CHUNKS
    half = width // 2
    quarter = half // 2
    part = quarter // Y
    strip = part // 2
    depth = domain // 2

    def ao_at(c, dz):
        return c * RING + lax.rem(z + dz + RING, RING)

    up, down, across = ao_at(col, 1), ao_at(col, -1), ao_at(1 - col, 0)

    def send(src, dst, send_sem, recv_sem, occ_to, ao_to):
        pltpu.make_async_remote_copy(
            src_ref=src, dst_ref=dst, send_sem=send_sem, recv_sem=recv_sem,
            device_id={"occ": occ_to, "ao": ao_to}, device_id_type=MESH,
        ).start()

    def chunk(slot, k):
        return held.at[slot, pl.ds(k * rows, rows), :]

    def send_chunk(src_slot, dst_slot, k, send_sem, to):
        send(chunk(src_slot, k), chunk(dst_slot, k), send_sem, chunk_sem.at[dst_slot, k], occ, to)

    def wait_chunk(slot, k):
        wait_for(chunk(slot, k), chunk_sem.at[slot, k])

    for load in loads:
        load.wait()
    for k in range(0, width, block):
        for s in range(slots):
            value = lax.dot_general(
                metric[blocks_ref[0, s]], ints[pl.ds(s * block, block), pl.ds(k, block)],
                (((1,), (0,)), ((), ())), preferred_element_type=F32,
            )
            live = jnp.full(value.shape, len_ref[0], jnp.int32) > s
            value = jnp.where(live, value, 0.0)
            held[2, pl.ds(k, block), pl.ds(s * block, block)] = value.T.astype(BF16)
        if k == 0:
            pl.semaphore_wait(barrier, n_occ + n_ao - 2)
        for m in range(k // rows, (k + block) // rows):
            send_chunk(2, 1, m, own_sem.at[0], up)
            send_chunk(2, 3, m, own_sem.at[1], down)

    groups, unit = [], 0
    upper = z // (RING // 2)
    for plan in PLAN:
        group = []
        for entry in plan:
            whole = (0, domain)
            if entry == "opposite":
                group.append((
                    unit, 1, 4 - 4 * upper, upper, 4 * upper, whole,
                    ao_at(col, 2 - 4 * upper), ao_at(col, 4 * upper - 2), True, 0,
                ))
            elif entry == "across":
                group.append((
                    unit, 2, 6 * col, 0, 6 - 2 * col, (pl.multiple_of(col * depth, depth), depth),
                    ao_at(0, -2), ao_at(1, 2), True, col,
                ))
            else:
                i, t, other, both, first, n = entry
                group.append((
                    unit, n, i + 2, first, t + 4 if other else t + 2, whole,
                    ao_at(col, i), ao_at(1 - col if other else col, t), both, 0,
                ))
            unit += group[-1][1]
        groups.append(group)

    def span(g):
        lo = groups[g][0][0]
        return pl.ds(lo, groups[g][-1][0] + groups[g][-1][1] - lo)

    def units(g):
        at = span(g)
        return range(at.start, at.start + at.size)

    def multiply(g):
        for u, n, left, first, right, (lo, size), *_ in groups[g]:
            for m in range(n):
                at = pl.ds(pl.multiple_of((first + m) * half, half), half)
                local[u + m] = lax.dot_general(
                    held[left, at, pl.ds(lo, size)], held[right, :, pl.ds(lo, size)], NT,
                    preferred_element_type=F32,
                )
                other = local[u + m, pl.ds(pl.multiple_of((1 - core) * quarter, quarter), quarter), :]
                give[u + m] = other.astype(BF16)
            send(
                give.at[pl.ds(u, n)], core_in.at[pl.ds(u, n)], core_send.at[g], core_recv.at[g],
                occ + 1 - 2 * core, ao,
            )

    def sum_cores(g):
        wait_for(core_in.at[span(g)], core_recv.at[g])
        for u in units(g):
            mine = local[u, pl.ds(pl.multiple_of(core * quarter, quarter), quarter), :]
            summed[u] = (mine + core_in[u].astype(F32)).astype(BF16)
        for k in (1, 3, 2):
            to = lax.rem(y + k, Y)
            send(
                summed.at[span(g), pl.ds(pl.multiple_of(to * part, part), part), :], y_in.at[k - 1, span(g)],
                y_send.at[g], y_recv.at[g], x * (2 * Y) + to * 2 + core, ao,
            )

    def sum_y(g):
        wait_for(y_in.at[:, span(g)], y_recv.at[g])
        for u in units(g):
            value = summed[u, pl.ds(pl.multiple_of(y * part, part), part), :].astype(F32)
            for k in range(Y - 1):
                value = value + y_in[k, u].astype(F32)
            y_sum[u] = value.astype(BF16)
        send(
            y_sum.at[span(g), pl.ds(pl.multiple_of((1 - x) * strip, strip), strip), :], x_in.at[span(g)],
            x_send.at[g], x_recv.at[g], (1 - x) * (2 * Y) + y * 2 + core, ao,
        )

    place = pl.ds(pl.multiple_of(core * quarter + (y * 2 + x) * strip, strip), strip)
    trips, number = [], 0
    for group in groups:
        trip = []
        for u, n, _, first, _, _, row_block, column_block, both, part_of in group:
            for occ_to, ao_to in ((column_block, row_block), (row_block, column_block))[: 1 + both]:
                mine = jnp.logical_and(occ_to == occ, ao_to == ao)
                trip.append((number, u, n, first, part_of, occ_to, ao_to, mine))
                number += 1
        trips.append(trip)

    def deliver(g):
        wait_for(x_in.at[span(g)], x_recv.at[g])
        for u in units(g):
            value = y_sum[u, pl.ds(pl.multiple_of(x * strip, strip), strip), :].astype(F32)
            final[u] = (value + x_in[u].astype(F32)).astype(BF16)
        for m, u, n, first, part_of, occ_to, ao_to, mine in trips[g]:
            src, dst = final.at[pl.ds(u, n)], owned.at[part_of, pl.ds(first, n), place, :]

            @pl.when(mine)
            def _():
                pltpu.make_async_copy(src, dst, end_recv.at[part_of]).start()

            @pl.when(jnp.logical_not(mine))
            def _():
                send(src, dst, end_send.at[m], end_recv.at[part_of], occ_to, ao_to)

    def pass_on(k):
        wait_chunk(1, k)
        send_chunk(1, 0, k, pass_sem.at[0], up)
        wait_chunk(3, k)
        send_chunk(3, 4, k, pass_sem.at[1], down)
        send_chunk(3, 5, k, pass_sem.at[2], across)

    def half_chunk(slot, k, which):
        return held.at[slot, pl.ds(k * rows, rows), pl.ds(pl.multiple_of(which * depth, depth), depth)]

    def pass_across(k):
        wait_chunk(0, k)
        wait_chunk(4, k)
        send(
            half_chunk(4 * col, k, 1 - col), half_chunk(6, k, 1 - col), pass_sem.at[3], chunk_sem.at[6, k],
            occ, across,
        )

    pass_on(0)
    multiply(0)
    pass_on(1)
    pair = lax.dot_general(
        coef_ref[...], held[2], (((1,), (0,)), ((), ())), preferred_element_type=F32
    )
    for s in range(slots):
        pair_in[ao, pl.ds(s, 1), :] = pair[0:1, s * block : (s + 1) * block]
    for k in range(1, n_ao):
        send(pair_in.at[ao], pair_in.at[ao], pair_send, pair_recv, occ, lax.rem(ao + k, n_ao))
    pass_on(2)
    sum_cores(0)
    pass_on(3)
    pass_on(4)
    pass_on(5)
    pass_on(6)
    pass_on(7)
    multiply(1)
    pass_across(0)
    sum_cores(1)
    pass_across(1)
    for k in range(CHUNKS):
        wait_chunk(5, k)
    multiply(2)
    pass_across(2)
    sum_cores(2)
    pass_across(3)
    multiply(3)
    sum_cores(3)
    pass_across(4)
    sum_y(0)
    sum_y(1)
    pass_across(5)
    pass_across(6)
    wait_for(pair_in.at[pl.ds(0, n_ao - 1)], pair_recv)
    term = pair_in[0]
    for k in range(1, n_ao):
        term = term + pair_in[k]
    term_in[occ, pl.ds(0, slots), :] = term
    for s in range(slots):
        term_in[occ, pl.ds(slots + s, 1), :] = jnp.full((1, block), blocks_ref[0, s], jnp.int32).astype(F32)
    for k in range(1, n_occ):
        send(term_in.at[occ], term_in.at[occ], term_send, term_recv, lax.rem(occ + k, n_occ), ao)

    pass_across(7)
    multiply(4)
    sum_y(2)
    sum_y(3)
    sum_cores(4)
    deliver(0)
    deliver(1)
    for k in range(CHUNKS):
        wait_for(half_chunk(6, k, col), chunk_sem.at[6, k])
    multiply(5)
    sum_cores(5)
    deliver(2)
    wait_for(term_in.at[pl.ds(0, n_occ - 1)], term_recv)
    terms = jnp.concatenate([term_in[i, 0:slots, :] for i in range(n_occ)], axis=0)
    numbers = jnp.concatenate([term_in[i, slots : 2 * slots, :] for i in range(n_occ)], axis=0)
    here = numbers == lax.broadcasted_iota(jnp.int32, numbers.shape, 1).astype(F32)
    full = lax.dot_general(
        here.astype(F32).T, terms, (((1,), (0,)), ((), ())),
        precision=lax.Precision.HIGHEST, preferred_element_type=F32,
    )
    dens_ref[...] = full[0 : dens_ref.shape[0]]

    deliver(3)
    sum_y(4)
    sum_y(5)
    deliver(4)
    deliver(5)
    difference = lax.rem(lax.rem(occ, RING) - z + RING, RING)
    far, same = difference == RING // 2, occ // RING == col
    below = jnp.logical_or(z < 2, z >= 2 + RING // 2)
    turned = jnp.logical_or(
        difference > RING // 2,
        jnp.logical_and(far, jnp.where(same, below.astype(jnp.int32), col) > 0),
    )
    wait_for(owned.at[0], end_recv.at[0])

    @pl.when(jnp.logical_and(far, jnp.logical_not(same)))
    def _():
        wait_for(owned.at[1], end_recv.at[1])
        owned[0] = (owned[0].astype(F32) + owned[1].astype(F32)).astype(BF16)

    @pl.when(turned)
    def _():
        out_ref[...] = owned[0].reshape(width, width).astype(F32).T.astype(BF16)

    @pl.when(jnp.logical_not(turned))
    def _():
        out_ref[...] = owned[0].reshape(width, width)

    wait_for(held.at[2], own_sem.at[0])
    wait_for(held.at[2], own_sem.at[1])
    for n in range(3):
        wait_for(held.at[0], pass_sem.at[n])
    wait_for(held.at[6, :, pl.ds(0, depth)], pass_sem.at[3])
    for g in range(len(PLAN)):
        wait_for(give.at[span(g)], core_send.at[g])
        wait_for(y_in.at[:, span(g)], y_send.at[g])
        wait_for(x_in.at[span(g)], x_send.at[g])
    wait_for(pair_in.at[pl.ds(0, n_ao - 1)], pair_send)
    wait_for(term_in.at[pl.ds(0, n_occ - 1)], term_send)
    for trip in trips:
        for m, u, n, *_, mine in trip:
            @pl.when(jnp.logical_not(mine))
            def _():
                wait_for(final.at[pl.ds(u, n)], end_send.at[m])


def on_device(coef, half_ints, metric_inv, dom_blocks, dom_len):
    _, domain, width = half_ints.shape
    fit_blocks, block, _ = metric_inv.shape
    slots = domain // block
    half = width // 2
    quarter = half // 2
    part = quarter // Y
    smem = pl.BlockSpec(memory_space=pltpu.SMEM)
    vmem = pl.BlockSpec(memory_space=pltpu.VMEM)
    hbm = pl.BlockSpec(memory_space=pl.ANY)
    dma = pltpu.SemaphoreType.DMA
    per_group = dma((len(PLAN),))
    exchange, density = pl.pallas_call(
        kernel,
        out_shape=(
            jax.ShapeDtypeStruct((width, width), BF16),
            jax.ShapeDtypeStruct((fit_blocks, block), F32),
        ),
        in_specs=[smem, smem, vmem, hbm, hbm],
        out_specs=(vmem, vmem),
        scratch_shapes=[
            pltpu.VMEM((domain, width), BF16),
            pltpu.VMEM((fit_blocks, block, block), BF16),
            pltpu.VMEM((7, width, domain), BF16),
            pltpu.VMEM((UNITS, quarter, width), BF16),
            pltpu.VMEM((UNITS, quarter, width), BF16),
            pltpu.VMEM((UNITS, half, width), F32),
            pltpu.VMEM((UNITS, quarter, width), BF16),
            pltpu.VMEM((Y - 1, UNITS, part, width), BF16),
            pltpu.VMEM((UNITS, part, width), BF16),
            pltpu.VMEM((UNITS, part // 2, width), BF16),
            pltpu.VMEM((UNITS, part // 2, width), BF16),
            pltpu.VMEM((2, 2, half, width), BF16),
            pltpu.VMEM((16, slots, block), F32),
            pltpu.VMEM((16, 2 * slots, block), F32),
            dma((2,)), dma((2,)), dma((4,)), dma((7, CHUNKS)),
            per_group, per_group, per_group, per_group, per_group, per_group,
            dma((SENDS,)), dma((2,)), dma, dma, dma, dma,
        ],
        compiler_params=pltpu.CompilerParams(
            vmem_limit_bytes=56 * 1024 * 1024, has_side_effects=True, collective_id=0
        ),
        cost_estimate=pl.CostEstimate(
            flops=UNITS * width * width * domain, bytes_accessed=8 * 1024 * 1024, transcendentals=0
        ),
        name="exchange",
    )(dom_blocks, dom_len, coef.reshape(1, width), half_ints.reshape(domain, width), metric_inv)
    return exchange.astype(F32), density.reshape(fit_blocks * block)


def solution(mesh):
    in_specs = (P("ao", "occ"), P("occ", None, "ao"), P(), P("occ", None), P("occ"))
    out_specs = (P("ao", "occ"), P())
    return jax.shard_map(
        on_device, mesh=mesh, in_specs=in_specs, out_specs=out_specs, check_vma=False
    )
```

```python
import jax
import jax.numpy as jnp
from jax import lax
from jax.experimental import pallas as pl
from jax.experimental.pallas import tpu as pltpu
from jax.sharding import PartitionSpec as P

MESH = pl.DeviceIdType.MESH
F32, BF16 = jnp.float32, jnp.bfloat16
RING = 8
Y = 4
CHUNKS = 8
PLAN = (
    ((0, 0, 0, False, 0, 2),),
    ((0, 1, 0, True, 0, 2), (-1, 1, 0, True, 0, 2)),
    ((1, 1, 1, False, 0, 2), (0, 1, 1, True, 0, 2), (-1, 1, 1, True, 0, 2)),
    ((-2, 1, 0, True, 0, 1), (-2, 1, 1, True, 0, 1)),
    ((-2, 1, 0, True, 1, 1), "opposite", (-2, 1, 1, True, 1, 1)),
    ("across",),
)
UNITS, SENDS, RUNS = 19, 22, 8
NT = (((1,), (1,)), ((), ()))


def wait_for(ref, sem):
    pltpu.make_async_copy(ref, ref, sem).wait()


def kernel(
    blocks_ref, len_ref, coef_ref, ints_hbm, metric_hbm,
    out_ref, dens_ref,
    ints, metric, held, give, core_in, local, summed, y_in, y_sum, x_in, final, owned, pair_in, term_in,
    load_sem, own_sem, pass_sem, chunk_sem, core_send, core_recv, y_send, y_recv, x_send, x_recv,
    end_send, end_recv, pair_send, pair_recv, term_send, term_recv,
):
    occ, ao = lax.axis_index("occ"), lax.axis_index("ao")
    n_occ, n_ao = term_in.shape[0], pair_in.shape[0]
    barrier = pltpu.get_barrier_semaphore()
    for k in range(1, n_occ):
        pl.semaphore_signal(
            barrier, inc=1, device_id={"occ": lax.rem(occ + k, n_occ), "ao": ao}, device_id_type=MESH
        )
    for k in range(1, n_ao):
        pl.semaphore_signal(
            barrier, inc=1, device_id={"occ": occ, "ao": lax.rem(ao + k, n_ao)}, device_id_type=MESH
        )
    loads = (
        pltpu.make_async_copy(metric_hbm, metric, load_sem.at[0]),
        pltpu.make_async_copy(ints_hbm, ints, load_sem.at[1]),
    )
    for load in loads:
        load.start()

    col, z = ao // RING, lax.rem(ao, RING)
    core = lax.rem(occ, 2)
    y, x = lax.rem(occ // 2, Y), occ // (2 * Y)
    width, domain = held.shape[1], held.shape[2]
    block = metric.shape[1]
    slots = domain // block
    rows = width // CHUNKS
    half = width // 2
    quarter = half // 2
    part = quarter // Y
    depth = domain // 2

    def ao_at(c, dz):
        return c * RING + lax.rem(z + dz + RING, RING)

    up, down, across = ao_at(col, 1), ao_at(col, -1), ao_at(1 - col, 0)

    def send(src, dst, send_sem, recv_sem, occ_to, ao_to):
        pltpu.make_async_remote_copy(
            src_ref=src, dst_ref=dst, send_sem=send_sem, recv_sem=recv_sem,
            device_id={"occ": occ_to, "ao": ao_to}, device_id_type=MESH,
        ).start()

    def chunk(slot, k):
        return held.at[slot, pl.ds(k * rows, rows), :]

    def send_chunk(src_slot, dst_slot, k, send_sem, to):
        send(chunk(src_slot, k), chunk(dst_slot, k), send_sem, chunk_sem.at[dst_slot, k], occ, to)

    def wait_chunk(slot, k):
        wait_for(chunk(slot, k), chunk_sem.at[slot, k])

    for load in loads:
        load.wait()
    for k in range(0, width, block):
        for s in range(slots):
            value = lax.dot_general(
                metric[blocks_ref[0, s]], ints[pl.ds(s * block, block), pl.ds(k, block)],
                (((1,), (0,)), ((), ())), preferred_element_type=F32,
            )
            live = jnp.full(value.shape, len_ref[0], jnp.int32) > s
            value = jnp.where(live, value, 0.0)
            held[2, pl.ds(k, block), pl.ds(s * block, block)] = value.T.astype(BF16)
        if k == 0:
            pl.semaphore_wait(barrier, n_occ + n_ao - 2)
        for m in range(k // rows, (k + block) // rows):
            send_chunk(2, 1, m, own_sem.at[0], up)
            send_chunk(2, 3, m, own_sem.at[1], down)

    groups, unit = [], 0
    upper = z // (RING // 2)
    for plan in PLAN:
        group = []
        for entry in plan:
            whole = (0, domain)
            if entry == "opposite":
                group.append((
                    unit, 1, 4 - 4 * upper, upper, 4 * upper, whole,
                    ao_at(col, 2 - 4 * upper), ao_at(col, 4 * upper - 2), True, 0, 0,
                ))
            elif entry == "across":
                group.append((
                    unit, 2, 6 * col, 0, 6 - 2 * col, (pl.multiple_of(col * depth, depth), depth),
                    ao_at(0, -2), ao_at(1, 2), True, col, 1,
                ))
            else:
                i, t, other, both, first, n = entry
                group.append((
                    unit, n, i + 2, first, t + 4 if other else t + 2, whole,
                    ao_at(col, i), ao_at(1 - col if other else col, t), both, 0, other,
                ))
            unit += group[-1][1]
        groups.append(group)

    def span(g):
        lo = groups[g][0][0]
        return pl.ds(lo, groups[g][-1][0] + groups[g][-1][1] - lo)

    def units(g):
        at = span(g)
        return range(at.start, at.start + at.size)

    def multiply(g):
        for u, n, left, first, right, (lo, size), *_ in groups[g]:
            for m in range(n):
                at = pl.ds(pl.multiple_of((first + m) * half, half), half)
                local[u + m] = lax.dot_general(
                    held[left, at, pl.ds(lo, size)], held[right, :, pl.ds(lo, size)], NT,
                    preferred_element_type=F32,
                )
                other = local[u + m, pl.ds(pl.multiple_of((1 - core) * quarter, quarter), quarter), :]
                give[u + m] = other.astype(BF16)
            send(
                give.at[pl.ds(u, n)], core_in.at[pl.ds(u, n)], core_send.at[g], core_recv.at[g],
                occ + 1 - 2 * core, ao,
            )

    def sum_cores(g):
        wait_for(core_in.at[span(g)], core_recv.at[g])
        for u in units(g):
            mine = local[u, pl.ds(pl.multiple_of(core * quarter, quarter), quarter), :]
            summed[u] = (mine + core_in[u].astype(F32)).astype(BF16)
        for k in (1, 3, 2):
            to = lax.rem(y + k, Y)
            send(
                summed.at[span(g), pl.ds(pl.multiple_of(to * part, part), part), :], y_in.at[k - 1, span(g)],
                y_send.at[g], y_recv.at[g], x * (2 * Y) + to * 2 + core, ao,
            )

    def sum_y(g):
        wait_for(y_in.at[:, span(g)], y_recv.at[g])
        for u in units(g):
            value = summed[u, pl.ds(pl.multiple_of(y * part, part), part), :].astype(F32)
            for k in range(Y - 1):
                value = value + y_in[k, u].astype(F32)
            y_sum[u] = value.astype(BF16)
        for r, at, keeper, _ in runs[g]:
            @pl.when(x != keeper)
            def _():
                send(
                    y_sum.at[at], x_in.at[at], x_send.at[r], x_recv.at[r], (1 - x) * (2 * Y) + y * 2 + core, ao,
                )

    place = pl.ds(pl.multiple_of(core * quarter + y * part, part), part)
    runs, run, number = [], 0, 0
    for group in groups:
        of_group = []
        for other in (0, 1):
            trip, first_unit, n_units = [], None, 0
            for u, n, _, first, _, _, row_block, column_block, both, part_of, kind in group:
                if kind != other:
                    continue
                first_unit = u if first_unit is None else first_unit
                n_units += n
                for occ_to, ao_to in ((column_block, row_block), (row_block, column_block))[: 1 + both]:
                    mine = jnp.logical_and(occ_to == occ, ao_to == ao)
                    trip.append((number, u, n, first, part_of, occ_to, ao_to, mine))
                    number += 1
            if trip:
                of_group.append((run, pl.ds(first_unit, n_units), 1 - col if other else col, trip))
                run += 1
        runs.append(of_group)

    def deliver(g):
        for r, at, keeper, trip in runs[g]:
            @pl.when(x == keeper)
            def _():
                wait_for(x_in.at[at], x_recv.at[r])
                for u in range(at.start, at.start + at.size):
                    final[u] = (y_sum[u].astype(F32) + x_in[u].astype(F32)).astype(BF16)
                for m, u, n, first, part_of, occ_to, ao_to, mine in trip:
                    src, dst = final.at[pl.ds(u, n)], owned.at[part_of, pl.ds(first, n), place, :]

                    @pl.when(mine)
                    def _():
                        pltpu.make_async_copy(src, dst, end_recv.at[part_of]).start()

                    @pl.when(jnp.logical_not(mine))
                    def _():
                        send(src, dst, end_send.at[m], end_recv.at[part_of], occ_to, ao_to)

    def pass_on(k):
        wait_chunk(1, k)
        send_chunk(1, 0, k, pass_sem.at[0], up)
        wait_chunk(3, k)
        send_chunk(3, 4, k, pass_sem.at[1], down)
        send_chunk(3, 5, k, pass_sem.at[2], across)

    def half_chunk(slot, k, which):
        return held.at[slot, pl.ds(k * rows, rows), pl.ds(pl.multiple_of(which * depth, depth), depth)]

    def pass_across(k):
        wait_chunk(0, k)
        wait_chunk(4, k)
        send(
            half_chunk(4 * col, k, 1 - col), half_chunk(6, k, 1 - col), pass_sem.at[3], chunk_sem.at[6, k],
            occ, across,
        )

    pass_on(0)
    multiply(0)
    pass_on(1)
    pair = lax.dot_general(
        coef_ref[...], held[2], (((1,), (0,)), ((), ())), preferred_element_type=F32
    )
    for s in range(slots):
        pair_in[ao, pl.ds(s, 1), :] = pair[0:1, s * block : (s + 1) * block]
    for k in range(1, n_ao):
        send(pair_in.at[ao], pair_in.at[ao], pair_send, pair_recv, occ, lax.rem(ao + k, n_ao))
    pass_on(2)
    sum_cores(0)
    pass_on(3)
    pass_on(4)
    pass_on(5)
    pass_on(6)
    pass_on(7)
    multiply(1)
    pass_across(0)
    sum_cores(1)
    sum_y(0)
    pass_across(1)
    for k in range(CHUNKS):
        wait_chunk(5, k)
    multiply(2)
    pass_across(2)
    sum_cores(2)
    pass_across(3)
    multiply(3)
    sum_cores(3)
    pass_across(4)
    sum_y(1)
    deliver(0)
    pass_across(5)
    sum_y(2)
    pass_across(6)
    deliver(1)
    wait_for(pair_in.at[pl.ds(0, n_ao - 1)], pair_recv)
    term = pair_in[0]
    for k in range(1, n_ao):
        term = term + pair_in[k]
    term_in[occ, pl.ds(0, slots), :] = term
    for s in range(slots):
        term_in[occ, pl.ds(slots + s, 1), :] = jnp.full((1, block), blocks_ref[0, s], jnp.int32).astype(F32)
    for k in range(1, n_occ):
        send(term_in.at[occ], term_in.at[occ], term_send, term_recv, lax.rem(occ + k, n_occ), ao)

    pass_across(7)
    multiply(4)
    sum_y(3)
    sum_cores(4)
    deliver(2)
    for k in range(CHUNKS):
        wait_for(half_chunk(6, k, col), chunk_sem.at[6, k])
    multiply(5)
    sum_cores(5)
    deliver(3)
    wait_for(term_in.at[pl.ds(0, n_occ - 1)], term_recv)
    terms = jnp.concatenate([term_in[i, 0:slots, :] for i in range(n_occ)], axis=0)
    numbers = jnp.concatenate([term_in[i, slots : 2 * slots, :] for i in range(n_occ)], axis=0)
    here = numbers == lax.broadcasted_iota(jnp.int32, numbers.shape, 1).astype(F32)
    full = lax.dot_general(
        here.astype(F32).T, terms, (((1,), (0,)), ((), ())),
        precision=lax.Precision.HIGHEST, preferred_element_type=F32,
    )
    dens_ref[...] = full[0 : dens_ref.shape[0]]

    sum_y(4)
    sum_y(5)
    deliver(4)
    deliver(5)
    difference = lax.rem(lax.rem(occ, RING) - z + RING, RING)
    far, same = difference == RING // 2, occ // RING == col
    below = jnp.logical_or(z < 2, z >= 2 + RING // 2)
    turned = jnp.logical_or(
        difference > RING // 2,
        jnp.logical_and(far, jnp.where(same, below.astype(jnp.int32), col) > 0),
    )
    wait_for(owned.at[0], end_recv.at[0])

    @pl.when(jnp.logical_and(far, jnp.logical_not(same)))
    def _():
        wait_for(owned.at[1], end_recv.at[1])
        owned[0] = (owned[0].astype(F32) + owned[1].astype(F32)).astype(BF16)

    @pl.when(turned)
    def _():
        out_ref[...] = owned[0].reshape(width, width).astype(F32).T.astype(BF16)

    @pl.when(jnp.logical_not(turned))
    def _():
        out_ref[...] = owned[0].reshape(width, width)

    wait_for(held.at[2], own_sem.at[0])
    wait_for(held.at[2], own_sem.at[1])
    for n in range(3):
        wait_for(held.at[0], pass_sem.at[n])
    wait_for(held.at[6, :, pl.ds(0, depth)], pass_sem.at[3])
    for g in range(len(PLAN)):
        wait_for(give.at[span(g)], core_send.at[g])
        wait_for(y_in.at[:, span(g)], y_send.at[g])
    wait_for(pair_in.at[pl.ds(0, n_ao - 1)], pair_send)
    wait_for(term_in.at[pl.ds(0, n_occ - 1)], term_send)
    for of_group in runs:
        for r, at, keeper, trip in of_group:
            @pl.when(x != keeper)
            def _():
                wait_for(x_in.at[at], x_send.at[r])

            for m, u, n, *_, mine in trip:
                @pl.when(jnp.logical_and(x == keeper, jnp.logical_not(mine)))
                def _():
                    wait_for(final.at[pl.ds(u, n)], end_send.at[m])


def widen(block_ref, dens_ref, out_ref, dens_out_ref):
    out_ref[...] = block_ref[...].astype(F32)
    dens_out_ref[...] = dens_ref[...]


def on_device(coef, half_ints, metric_inv, dom_blocks, dom_len):
    _, domain, width = half_ints.shape
    fit_blocks, block, _ = metric_inv.shape
    slots = domain // block
    half = width // 2
    quarter = half // 2
    part = quarter // Y
    smem = pl.BlockSpec(memory_space=pltpu.SMEM)
    vmem = pl.BlockSpec(memory_space=pltpu.VMEM)
    hbm = pl.BlockSpec(memory_space=pl.ANY)
    dma = pltpu.SemaphoreType.DMA
    per_group = dma((len(PLAN),))
    exchange, density = pl.pallas_call(
        kernel,
        out_shape=(
            jax.ShapeDtypeStruct((width, width), BF16),
            jax.ShapeDtypeStruct((fit_blocks, block), F32),
        ),
        in_specs=[smem, smem, vmem, hbm, hbm],
        out_specs=(vmem, vmem),
        scratch_shapes=[
            pltpu.VMEM((domain, width), BF16),
            pltpu.VMEM((fit_blocks, block, block), BF16),
            pltpu.VMEM((7, width, domain), BF16),
            pltpu.VMEM((UNITS, quarter, width), BF16),
            pltpu.VMEM((UNITS, quarter, width), BF16),
            pltpu.VMEM((UNITS, half, width), F32),
            pltpu.VMEM((UNITS, quarter, width), BF16),
            pltpu.VMEM((Y - 1, UNITS, part, width), BF16),
            pltpu.VMEM((UNITS, part, width), BF16),
            pltpu.VMEM((UNITS, part, width), BF16),
            pltpu.VMEM((UNITS, part, width), BF16),
            pltpu.VMEM((2, 2, half, width), BF16),
            pltpu.VMEM((16, slots, block), F32),
            pltpu.VMEM((16, 2 * slots, block), F32),
            dma((2,)), dma((2,)), dma((4,)), dma((7, CHUNKS)),
            per_group, per_group, per_group, per_group, dma((RUNS,)), dma((RUNS,)),
            dma((SENDS,)), dma((2,)), dma, dma, dma, dma,
        ],
        compiler_params=pltpu.CompilerParams(
            vmem_limit_bytes=56 * 1024 * 1024, has_side_effects=True, collective_id=0
        ),
        cost_estimate=pl.CostEstimate(
            flops=UNITS * width * width * domain, bytes_accessed=8 * 1024 * 1024, transcendentals=0
        ),
        name="exchange",
    )(dom_blocks, dom_len, coef.reshape(1, width), half_ints.reshape(domain, width), metric_inv)
    exchange, density = pl.pallas_call(
        widen,
        out_shape=(
            jax.ShapeDtypeStruct((width, width), F32),
            jax.ShapeDtypeStruct((fit_blocks, block), F32),
        ),
        in_specs=[vmem, vmem],
        out_specs=(vmem, vmem),
        name="widen",
    )(exchange, density)
    return exchange, density.reshape(fit_blocks * block)


def solution(mesh):
    in_specs = (P("ao", "occ"), P("occ", None, "ao"), P(), P("occ", None), P("occ"))
    out_specs = (P("ao", "occ"), P())
    return jax.shard_map(
        on_device, mesh=mesh, in_specs=in_specs, out_specs=out_specs, check_vma=False
    )
```

```python
import jax
import jax.numpy as jnp
from jax import lax
from jax.experimental import pallas as pl
from jax.experimental.pallas import tpu as pltpu
from jax.sharding import PartitionSpec as P

MESH = pl.DeviceIdType.MESH
F32, BF16 = jnp.float32, jnp.bfloat16
RING = 8
Y = 4
CHUNKS = 8
PLAN = (
    ((0, 0, 0, False, 0, 2),),
    ((0, 1, 0, True, 0, 2), (-1, 1, 0, True, 0, 2)),
    ((1, 1, 1, False, 0, 2), (0, 1, 1, True, 0, 2), (-1, 1, 1, True, 0, 2)),
    ((-2, 1, 0, True, 0, 1), (-2, 1, 1, True, 0, 1)),
    ((-2, 1, 0, True, 1, 1), "opposite", (-2, 1, 1, True, 1, 1)),
    ("across",),
)
UNITS, SENDS, RUNS = 19, 22, 8
NT = (((1,), (1,)), ((), ()))


def wait_for(ref, sem):
    pltpu.make_async_copy(ref, ref, sem).wait()


def kernel(
    blocks_ref, len_ref, coef_ref, ints_hbm, metric_hbm,
    out_ref, dens_ref,
    ints, metric, held, give, core_in, local, summed, y_in, y_sum, x_in, final, owned, pair_in, term_in,
    load_sem, own_sem, pass_sem, chunk_sem, core_send, core_recv, y_send, y_recv, x_send, x_recv,
    end_send, end_recv, pair_send, pair_recv, term_send, term_recv,
):
    occ, ao = lax.axis_index("occ"), lax.axis_index("ao")
    n_occ, n_ao = term_in.shape[0], pair_in.shape[0]
    barrier = pltpu.get_barrier_semaphore()
    for k in range(1, n_occ):
        pl.semaphore_signal(
            barrier, inc=1, device_id={"occ": lax.rem(occ + k, n_occ), "ao": ao}, device_id_type=MESH
        )
    for k in range(1, n_ao):
        pl.semaphore_signal(
            barrier, inc=1, device_id={"occ": occ, "ao": lax.rem(ao + k, n_ao)}, device_id_type=MESH
        )
    loads = (
        pltpu.make_async_copy(metric_hbm, metric, load_sem.at[0]),
        pltpu.make_async_copy(ints_hbm, ints, load_sem.at[1]),
    )
    for load in loads:
        load.start()

    col, z = ao // RING, lax.rem(ao, RING)
    core = lax.rem(occ, 2)
    y, x = lax.rem(occ // 2, Y), occ // (2 * Y)
    width, domain = held.shape[1], held.shape[2]
    block = metric.shape[1]
    slots = domain // block
    rows = width // CHUNKS
    half = width // 2
    quarter = half // 2
    part = quarter // Y
    depth = domain // 2

    def ao_at(c, dz):
        return c * RING + lax.rem(z + dz + RING, RING)

    up, down, across = ao_at(col, 1), ao_at(col, -1), ao_at(1 - col, 0)

    def send(src, dst, send_sem, recv_sem, occ_to, ao_to):
        pltpu.make_async_remote_copy(
            src_ref=src, dst_ref=dst, send_sem=send_sem, recv_sem=recv_sem,
            device_id={"occ": occ_to, "ao": ao_to}, device_id_type=MESH,
        ).start()

    def chunk(slot, k):
        return held.at[slot, pl.ds(k * rows, rows), :]

    def send_chunk(src_slot, dst_slot, k, send_sem, to):
        send(chunk(src_slot, k), chunk(dst_slot, k), send_sem, chunk_sem.at[dst_slot, k], occ, to)

    def wait_chunk(slot, k):
        wait_for(chunk(slot, k), chunk_sem.at[slot, k])

    for load in loads:
        load.wait()
    for k in range(0, width, block):
        for s in range(slots):
            value = lax.dot_general(
                metric[blocks_ref[0, s]], ints[pl.ds(s * block, block), pl.ds(k, block)],
                (((1,), (0,)), ((), ())), preferred_element_type=F32,
            )
            live = jnp.full(value.shape, len_ref[0], jnp.int32) > s
            value = jnp.where(live, value, 0.0)
            held[2, pl.ds(k, block), pl.ds(s * block, block)] = value.T.astype(BF16)
        if k == 0:
            pl.semaphore_wait(barrier, n_occ + n_ao - 2)
        for m in range(k // rows, (k + block) // rows):
            send_chunk(2, 1, m, own_sem.at[0], up)
            send_chunk(2, 3, m, own_sem.at[1], down)

    groups, unit = [], 0
    upper = z // (RING // 2)
    for plan in PLAN:
        group = []
        for entry in plan:
            whole = (0, domain)
            if entry == "opposite":
                group.append((
                    unit, 1, 4 - 4 * upper, upper, 4 * upper, whole,
                    ao_at(col, 2 - 4 * upper), ao_at(col, 4 * upper - 2), True, 0, 0,
                ))
            elif entry == "across":
                group.append((
                    unit, 2, 6 * col, 0, 6 - 2 * col, (pl.multiple_of(col * depth, depth), depth),
                    ao_at(0, -2), ao_at(1, 2), True, col, 1,
                ))
            else:
                i, t, other, both, first, n = entry
                group.append((
                    unit, n, i + 2, first, t + 4 if other else t + 2, whole,
                    ao_at(col, i), ao_at(1 - col if other else col, t), both, 0, other,
                ))
            unit += group[-1][1]
        groups.append(group)

    def span(g):
        lo = groups[g][0][0]
        return pl.ds(lo, groups[g][-1][0] + groups[g][-1][1] - lo)

    def units(g):
        at = span(g)
        return range(at.start, at.start + at.size)

    def multiply(g):
        for u, n, left, first, right, (lo, size), *_ in groups[g]:
            for m in range(n):
                at = pl.ds(pl.multiple_of((first + m) * half, half), half)
                local[u + m] = lax.dot_general(
                    held[left, at, pl.ds(lo, size)], held[right, :, pl.ds(lo, size)], NT,
                    preferred_element_type=F32,
                )
                other = local[u + m, pl.ds(pl.multiple_of((1 - core) * quarter, quarter), quarter), :]
                give[u + m] = other.astype(BF16)
            send(
                give.at[pl.ds(u, n)], core_in.at[pl.ds(u, n)], core_send.at[g], core_recv.at[g],
                occ + 1 - 2 * core, ao,
            )

    def sum_cores(g):
        wait_for(core_in.at[span(g)], core_recv.at[g])
        for u in units(g):
            mine = local[u, pl.ds(pl.multiple_of(core * quarter, quarter), quarter), :]
            summed[u] = (mine + core_in[u].astype(F32)).astype(BF16)
        for k in (2, 1, 3):
            to = lax.rem(y + k, Y)
            send(
                summed.at[span(g), pl.ds(pl.multiple_of(to * part, part), part), :], y_in.at[k - 1, span(g)],
                y_send.at[g], y_recv.at[g], x * (2 * Y) + to * 2 + core, ao,
            )

    def sum_y(g):
        wait_for(y_in.at[:, span(g)], y_recv.at[g])
        for u in units(g):
            value = summed[u, pl.ds(pl.multiple_of(y * part, part), part), :].astype(F32)
            for k in range(Y - 1):
                value = value + y_in[k, u].astype(F32)
            y_sum[u] = value.astype(BF16)
        for r, at, keeper, _ in runs[g]:
            @pl.when(x != keeper)
            def _():
                send(
                    y_sum.at[at], x_in.at[at], x_send.at[r], x_recv.at[r], (1 - x) * (2 * Y) + y * 2 + core, ao,
                )

    place = pl.ds(pl.multiple_of(core * quarter + y * part, part), part)
    runs, run, number = [], 0, 0
    for group in groups:
        of_group = []
        for other in (0, 1):
            trip, first_unit, n_units = [], None, 0
            for u, n, _, first, _, _, row_block, column_block, both, part_of, kind in group:
                if kind != other:
                    continue
                first_unit = u if first_unit is None else first_unit
                n_units += n
                for occ_to, ao_to in ((column_block, row_block), (row_block, column_block))[: 1 + both]:
                    mine = jnp.logical_and(occ_to == occ, ao_to == ao)
                    trip.append((number, u, n, first, part_of, occ_to, ao_to, mine))
                    number += 1
            if trip:
                of_group.append((run, pl.ds(first_unit, n_units), 1 - col if other else col, trip))
                run += 1
        runs.append(of_group)

    def deliver(g):
        for r, at, keeper, trip in runs[g]:
            @pl.when(x == keeper)
            def _():
                wait_for(x_in.at[at], x_recv.at[r])
                for u in range(at.start, at.start + at.size):
                    final[u] = (y_sum[u].astype(F32) + x_in[u].astype(F32)).astype(BF16)
                for m, u, n, first, part_of, occ_to, ao_to, mine in trip:
                    src, dst = final.at[pl.ds(u, n)], owned.at[part_of, pl.ds(first, n), place, :]

                    @pl.when(mine)
                    def _():
                        pltpu.make_async_copy(src, dst, end_recv.at[part_of]).start()

                    @pl.when(jnp.logical_not(mine))
                    def _():
                        send(src, dst, end_send.at[m], end_recv.at[part_of], occ_to, ao_to)

    def pass_on(k):
        wait_chunk(1, k)
        send_chunk(1, 0, k, pass_sem.at[0], up)
        wait_chunk(3, k)
        send_chunk(3, 4, k, pass_sem.at[1], down)
        send_chunk(3, 5, k, pass_sem.at[2], across)

    def half_chunk(slot, k, which):
        return held.at[slot, pl.ds(k * rows, rows), pl.ds(pl.multiple_of(which * depth, depth), depth)]

    def pass_across(k):
        wait_chunk(0, k)
        wait_chunk(4, k)
        send(
            half_chunk(4 * col, k, 1 - col), half_chunk(6, k, 1 - col), pass_sem.at[3], chunk_sem.at[6, k],
            occ, across,
        )

    pass_on(0)
    multiply(0)
    pass_on(1)
    pair = lax.dot_general(
        coef_ref[...], held[2], (((1,), (0,)), ((), ())), preferred_element_type=F32
    )
    for s in range(slots):
        pair_in[ao, pl.ds(s, 1), :] = pair[0:1, s * block : (s + 1) * block]
    for k in range(1, n_ao):
        send(pair_in.at[ao], pair_in.at[ao], pair_send, pair_recv, occ, lax.rem(ao + k, n_ao))
    pass_on(2)
    sum_cores(0)
    pass_on(3)
    pass_on(4)
    pass_on(5)
    pass_on(6)
    pass_on(7)
    multiply(1)
    pass_across(0)
    sum_cores(1)
    sum_y(0)
    pass_across(1)
    for k in range(CHUNKS):
        wait_chunk(5, k)
    multiply(2)
    pass_across(2)
    sum_cores(2)
    pass_across(3)
    multiply(3)
    sum_cores(3)
    pass_across(4)
    sum_y(1)
    deliver(0)
    pass_across(5)
    sum_y(2)
    pass_across(6)
    deliver(1)
    wait_for(pair_in.at[pl.ds(0, n_ao - 1)], pair_recv)
    term = pair_in[0]
    for k in range(1, n_ao):
        term = term + pair_in[k]
    term_in[occ, pl.ds(0, slots), :] = term
    for s in range(slots):
        term_in[occ, pl.ds(slots + s, 1), :] = jnp.full((1, block), blocks_ref[0, s], jnp.int32).astype(F32)
    for k in range(1, n_occ):
        send(term_in.at[occ], term_in.at[occ], term_send, term_recv, lax.rem(occ + k, n_occ), ao)

    pass_across(7)
    multiply(4)
    sum_y(3)
    sum_cores(4)
    deliver(2)
    for k in range(CHUNKS):
        wait_for(half_chunk(6, k, col), chunk_sem.at[6, k])
    multiply(5)
    sum_cores(5)
    deliver(3)
    wait_for(term_in.at[pl.ds(0, n_occ - 1)], term_recv)
    terms = jnp.concatenate([term_in[i, 0:slots, :] for i in range(n_occ)], axis=0)
    numbers = jnp.concatenate([term_in[i, slots : 2 * slots, :] for i in range(n_occ)], axis=0)
    here = numbers == lax.broadcasted_iota(jnp.int32, numbers.shape, 1).astype(F32)
    full = lax.dot_general(
        here.astype(F32).T, terms, (((1,), (0,)), ((), ())),
        precision=lax.Precision.HIGHEST, preferred_element_type=F32,
    )
    dens_ref[...] = full[0 : dens_ref.shape[0]]

    sum_y(4)
    sum_y(5)
    deliver(4)
    deliver(5)
    difference = lax.rem(lax.rem(occ, RING) - z + RING, RING)
    far, same = difference == RING // 2, occ // RING == col
    below = jnp.logical_or(z < 2, z >= 2 + RING // 2)
    turned = jnp.logical_or(
        difference > RING // 2,
        jnp.logical_and(far, jnp.where(same, below.astype(jnp.int32), col) > 0),
    )
    wait_for(owned.at[0], end_recv.at[0])

    @pl.when(jnp.logical_and(far, jnp.logical_not(same)))
    def _():
        wait_for(owned.at[1], end_recv.at[1])
        owned[0] = (owned[0].astype(F32) + owned[1].astype(F32)).astype(BF16)

    @pl.when(turned)
    def _():
        out_ref[...] = owned[0].reshape(width, width).astype(F32).T.astype(BF16)

    @pl.when(jnp.logical_not(turned))
    def _():
        out_ref[...] = owned[0].reshape(width, width)

    wait_for(held.at[2], own_sem.at[0])
    wait_for(held.at[2], own_sem.at[1])
    for n in range(3):
        wait_for(held.at[0], pass_sem.at[n])
    wait_for(held.at[6, :, pl.ds(0, depth)], pass_sem.at[3])
    for g in range(len(PLAN)):
        wait_for(give.at[span(g)], core_send.at[g])
        wait_for(y_in.at[:, span(g)], y_send.at[g])
    wait_for(pair_in.at[pl.ds(0, n_ao - 1)], pair_send)
    wait_for(term_in.at[pl.ds(0, n_occ - 1)], term_send)
    for of_group in runs:
        for r, at, keeper, trip in of_group:
            @pl.when(x != keeper)
            def _():
                wait_for(x_in.at[at], x_send.at[r])

            for m, u, n, *_, mine in trip:
                @pl.when(jnp.logical_and(x == keeper, jnp.logical_not(mine)))
                def _():
                    wait_for(final.at[pl.ds(u, n)], end_send.at[m])


def widen(block_ref, dens_ref, out_ref, dens_out_ref):
    out_ref[...] = block_ref[...].astype(F32)
    dens_out_ref[...] = dens_ref[...]


def on_device(coef, half_ints, metric_inv, dom_blocks, dom_len):
    _, domain, width = half_ints.shape
    fit_blocks, block, _ = metric_inv.shape
    slots = domain // block
    half = width // 2
    quarter = half // 2
    part = quarter // Y
    smem = pl.BlockSpec(memory_space=pltpu.SMEM)
    vmem = pl.BlockSpec(memory_space=pltpu.VMEM)
    hbm = pl.BlockSpec(memory_space=pl.ANY)
    dma = pltpu.SemaphoreType.DMA
    per_group = dma((len(PLAN),))
    exchange, density = pl.pallas_call(
        kernel,
        out_shape=(
            jax.ShapeDtypeStruct((width, width), BF16),
            jax.ShapeDtypeStruct((fit_blocks, block), F32),
        ),
        in_specs=[smem, smem, vmem, hbm, hbm],
        out_specs=(vmem, vmem),
        scratch_shapes=[
            pltpu.VMEM((domain, width), BF16),
            pltpu.VMEM((fit_blocks, block, block), BF16),
            pltpu.VMEM((7, width, domain), BF16),
            pltpu.VMEM((UNITS, quarter, width), BF16),
            pltpu.VMEM((UNITS, quarter, width), BF16),
            pltpu.VMEM((UNITS, half, width), F32),
            pltpu.VMEM((UNITS, quarter, width), BF16),
            pltpu.VMEM((Y - 1, UNITS, part, width), BF16),
            pltpu.VMEM((UNITS, part, width), BF16),
            pltpu.VMEM((UNITS, part, width), BF16),
            pltpu.VMEM((UNITS, part, width), BF16),
            pltpu.VMEM((2, 2, half, width), BF16),
            pltpu.VMEM((16, slots, block), F32),
            pltpu.VMEM((16, 2 * slots, block), F32),
            dma((2,)), dma((2,)), dma((4,)), dma((7, CHUNKS)),
            per_group, per_group, per_group, per_group, dma((RUNS,)), dma((RUNS,)),
            dma((SENDS,)), dma((2,)), dma, dma, dma, dma,
        ],
        compiler_params=pltpu.CompilerParams(
            vmem_limit_bytes=56 * 1024 * 1024, has_side_effects=True, collective_id=0
        ),
        cost_estimate=pl.CostEstimate(
            flops=UNITS * width * width * domain, bytes_accessed=8 * 1024 * 1024, transcendentals=0
        ),
        name="exchange",
    )(dom_blocks, dom_len, coef.reshape(1, width), half_ints.reshape(domain, width), metric_inv)
    exchange, density = pl.pallas_call(
        widen,
        out_shape=(
            jax.ShapeDtypeStruct((width, width), F32),
            jax.ShapeDtypeStruct((fit_blocks, block), F32),
        ),
        in_specs=[vmem, vmem],
        out_specs=(vmem, vmem),
        name="widen",
    )(exchange, density)
    return exchange, density.reshape(fit_blocks * block)


def solution(mesh):
    in_specs = (P("ao", "occ"), P("occ", None, "ao"), P(), P("occ", None), P("occ"))
    out_specs = (P("ao", "occ"), P())
    return jax.shard_map(
        on_device, mesh=mesh, in_specs=in_specs, out_specs=out_specs, check_vma=False
    )
```
